32 devices in a mesh: lon: 4 (over y, core), lat: 8 (over z, x).
Axes of the slice: x: 2, y: 2, z: 4, core: 2. Of those that a mesh axis runs over, the one named last changes fastest.
Arguments:
- grid: bfloat16 [12, 2, 2, 1024, 4096], P(None, None, None, 'lat', 'lon'), may hold values from -6 to 6
- legendre: bfloat16 [4, 256, 1024, 2, 512], P('lon', None, 'lat'), may hold values from -0.25 to 0.25
Outputs:
- spectral: float32 [4, 256, 8, 2, 2, 2, 512], P('lon', 'lat')
The draws below stay inside these ranges and needn't reach their ends.
All inputs are finite; a program needn't handle non-finite values.
Results may differ from the reference program's by a relative error of at most 0.0029.
Values sent between devices are 32-bit elements; how exact they have to be, the bound alone decides.
No kernel may reach another device: no remote copies, remote signals or barrier semaphores. Data moves between devices by JAX's collectives and lax.ppermute only.
A program may use at most 320 MiB of HBM per device.

```python
import math
import jax
import jax.numpy as jnp
import numpy as np
from jax import lax

NLON = 4096
WAVES = 1024
FIELDS = 12
LEV = 2
NHALF = 1024
WAVE_DEV = 256
N_LON = 4


def spiked(values, own_key, source, target, shards_of, factor):
    owner, partner = [(jnp.arange(values.shape[dim]) // (values.shape[dim] // shards_of)).reshape([-1 if axis == dim else 1 for axis in range(values.ndim)]) for dim in (source, target)]
    chosen = jax.random.permutation(own_key, shards_of)[partner]
    strong = (owner == chosen) | (owner == (partner + shards_of // 2) % shards_of)
    return jnp.where(strong, factor * values, values)


def levels(key, shape, split, smallest, largest):
    def one(dim, blocks):
        draws = jax.random.uniform(jax.random.fold_in(jax.random.fold_in(key, 6), dim), (blocks,), jnp.float32, smallest / len(split), largest / len(split))
        return jnp.repeat(jnp.exp(draws), shape[dim] // blocks).reshape((-1,) + (1,) * (len(shape) - dim - 1))

    gain = one(*split[0])
    for cut in split[1:]:
        gain = gain * one(*cut)
    return gain


def gaussian(rng, dims, scale, limit, shards=(), kind=jnp.bfloat16):
    entries = jax.random.normal(rng, dims, jnp.float32) * scale
    if len(shards) > 0:
        entries = levels(rng, dims, shards, -0.22, 0.18) * entries
    return jnp.clip(entries, min=-limit, max=limit).astype(kind)


def heavy_noise(stream_key, extent, width, reach, shards, heavy, held_as=jnp.bfloat16):
    values = width * jax.random.normal(stream_key, extent, jnp.float32)
    if shards:
        values = values * levels(stream_key, extent, shards, -0.22, 0.18)
    return jnp.clip(spiked(values, jax.random.fold_in(stream_key, 3), *heavy), -reach, reach).astype(held_as)


def setup_inputs(seed: int = 0) -> dict:
    key_list = jax.random.split(jax.random.key(seed), 3)
    return {
        "grid": gaussian(key_list[0], (FIELDS, LEV, 2, NHALF, NLON), 1.0, 6.0, ((3, 8), (4, 4))),
        "legendre": heavy_noise(key_list[1], (N_LON, WAVE_DEV, NHALF, 2, WAVES // 2), NHALF ** -0.5, 0.25, ((0, 4), (2, 8)), (2, 1, 8, 2.0)),
    }


adiabatic_exponent = 0.286

def tendency_fields(numeric_buffer_grid):
    eastward_flow_speed, poleward_flow_speed, local_spin_field, flow_spreading_rate = (numeric_buffer_grid[0], numeric_buffer_grid[1], numeric_buffer_grid[2], numeric_buffer_grid[3])
    kinetic_warmth_field, water_vapour_mixing = (numeric_buffer_grid[4], numeric_buffer_grid[5])
    warmth_eastward_slope, warmth_poleward_slope = (numeric_buffer_grid[6], numeric_buffer_grid[7])
    vapour_eastward_slope, vapour_poleward_slope = (numeric_buffer_grid[8], numeric_buffer_grid[9])
    ground_load_eastward_slope, ground_load_poleward_slope = (numeric_buffer_grid[10], numeric_buffer_grid[11])
    return jnp.stack([local_spin_field * poleward_flow_speed - kinetic_warmth_field * ground_load_eastward_slope, -local_spin_field * eastward_flow_speed - kinetic_warmth_field * ground_load_poleward_slope, eastward_flow_speed * poleward_flow_speed, -(eastward_flow_speed * warmth_eastward_slope + poleward_flow_speed * warmth_poleward_slope) + adiabatic_exponent * kinetic_warmth_field * flow_spreading_rate, -(eastward_flow_speed * vapour_eastward_slope + poleward_flow_speed * vapour_poleward_slope) - water_vapour_mixing * flow_spreading_rate, eastward_flow_speed * kinetic_warmth_field, poleward_flow_speed * kinetic_warmth_field, poleward_flow_speed * water_vapour_mixing], 0)

def reference(grid, legendre):
    devices = N_LON
    per_device = WAVES // devices
    order = np.arange(WAVES).reshape(per_device, devices).T

    def level_spectra(level_grid):
        tendencies = tendency_fields(level_grid.astype(jnp.float32))
        spectrum = jnp.fft.rfft(tendencies, axis=-1)[..., :WAVES] / math.sqrt(NLON)
        parts = jnp.stack([jnp.real(spectrum), jnp.imag(spectrum)], 3)
        return parts[..., order]
    spectra = lax.map(level_spectra, jnp.moveaxis(grid, 1, 0))
    northern = spectra[:, :, 0]
    southern = spectra[:, :, 1]
    folded = jnp.stack([northern + southern, northern - southern], 0).astype(jnp.bfloat16)
    moved = jnp.moveaxis(folded, 5, 0)

    def project(pair):
        section, weights = pair
        return jnp.einsum('elkjcs,sjeh->sklceh', section.astype(jnp.float32), weights.astype(jnp.float32))
    result = lax.map(project, (moved, legendre))
    wavenumber = jnp.asarray(order, dtype=jnp.int32)[:, :, None, None]
    degree = 2 * jnp.arange(WAVES // 2, dtype=jnp.int32)[None, None, None, :] + jnp.arange(2, dtype=jnp.int32)[None, None, :, None]
    inside = wavenumber + degree < WAVES
    return jnp.where(inside[:, :, None, None, None], result, jnp.zeros((), jnp.float32))
```

```python
import math

import jax
import jax.numpy as jnp
import numpy as np
from jax import lax
from jax.experimental import pallas as pl
from jax.experimental.pallas import tpu as pltpu
from jax.sharding import PartitionSpec as P


ADIABATIC = 0.286
LANES = 128
SPLIT = ((1, 1, 2), (2, 1, 1))
ROWS_CONTRACTED = (((1,), (1,)), ((), ()))


def tendency_kernel(grid_ref, high_ref, low_ref, scratch):
    pairs = grid_ref.shape[3]
    pieces = grid_ref.shape[4] // LANES

    def field(n):
        return [grid_ref[n, 0, h].astype(jnp.float32) for h in range(2)]

    u, v, zeta, div, temp, hum, temp_x, temp_y, hum_x, hum_y, press_x, press_y = [
        field(n) for n in range(12)
    ]
    formulas = [
        lambda h: zeta[h] * v[h] - temp[h] * press_x[h],
        lambda h: -zeta[h] * u[h] - temp[h] * press_y[h],
        lambda h: u[h] * v[h],
        lambda h: -(u[h] * temp_x[h] + v[h] * temp_y[h]) + ADIABATIC * temp[h] * div[h],
        lambda h: -(u[h] * hum_x[h] + v[h] * hum_y[h]) - hum[h] * div[h],
        lambda h: u[h] * temp[h],
        lambda h: v[h] * temp[h],
        lambda h: v[h] * hum[h],
    ]
    for t, formula in enumerate(formulas):
        north, south = formula(0), formula(1)
        even, odd = north + south, north - south
        for piece in range(pieces):
            lanes = slice(piece * LANES, (piece + 1) * LANES)
            place = t * pieces + piece
            scratch[place, pl.ds(0, pairs, stride=2), :] = even[:, lanes]
            scratch[place, pl.ds(1, pairs, stride=2), :] = odd[:, lanes]
            whole = scratch[place]
            high = whole.astype(jnp.bfloat16)
            high_ref[t, 0, :, lanes] = high
            low_ref[t, 0, :, lanes] = (whole - high.astype(jnp.float32)).astype(jnp.bfloat16)


def folded_tendencies(grid):
    fields, levels, hemispheres, pairs, longitudes = grid.shape
    width = min(256, longitudes)
    shape = jax.ShapeDtypeStruct((8, levels, 2 * pairs, longitudes), jnp.bfloat16)
    high, low = pl.pallas_call(
        tendency_kernel,
        grid=(levels, longitudes // width),
        in_specs=[
            pl.BlockSpec((fields, 1, hemispheres, pairs, width), lambda l, x: (0, l, 0, 0, x))
        ],
        out_specs=[pl.BlockSpec((8, 1, 2 * pairs, width), lambda l, x: (0, l, 0, x))] * 2,
        out_shape=(shape, shape),
        scratch_shapes=[pltpu.VMEM((8 * width // LANES, 2 * pairs, LANES), jnp.float32)],
        cost_estimate=pl.CostEstimate(
            flops=4 * grid.size, bytes_accessed=5 * grid.size, transcendentals=0
        ),
        name="tendencies",
    )(grid)
    rows = 8 * levels * 2 * pairs
    return high.reshape(rows, longitudes), low.reshape(rows, longitudes)


def product3(phase_high, phase_low, high, low):
    def one(a, b):
        return lax.dot_general(a, b, ROWS_CONTRACTED, preferred_element_type=jnp.float32)

    return one(phase_high, high) + (one(phase_high, low) + one(phase_low, high))


def first_fourier_kernel(ph_ref, pl_ref, high_ref, low_ref, out_ref):
    out_ref[...] = product3(ph_ref[...], pl_ref[...], high_ref[...], low_ref[...])


def second_fourier_kernel(ph_ref, pl_ref, high_ref, low_ref, came_ref, *out_refs):
    total = product3(ph_ref[...], pl_ref[...], high_ref[...], low_ref[...]) + came_ref[...]
    start = 0
    for out_ref in out_refs:
        rows = out_ref.shape[0]
        out_ref[...] = total[start : start + rows]
        start += rows


def fourier(phases, tendencies, came=None, parts=()):
    high, low = tendencies
    orders, longitudes = phases[0].shape
    rows = high.shape[0]
    block = min(512, rows)
    whole = pl.BlockSpec((orders, longitudes), lambda r: (0, 0))
    part = pl.BlockSpec((block, longitudes), lambda r: (r, 0))

    def columns(count):
        return pl.BlockSpec((count, block), lambda r: (0, r))

    cost = pl.CostEstimate(
        flops=6 * orders * longitudes * rows,
        bytes_accessed=4 * rows * (longitudes + orders),
        transcendentals=0,
    )
    if came is None:
        return pl.pallas_call(
            first_fourier_kernel,
            grid=(rows // block,),
            in_specs=[whole, whole, part, part],
            out_specs=columns(orders),
            out_shape=jax.ShapeDtypeStruct((orders, rows), jnp.float32),
            cost_estimate=cost,
            name="fourier_first",
        )(*phases, high, low)
    return pl.pallas_call(
        second_fourier_kernel,
        grid=(rows // block,),
        in_specs=[whole, whole, part, part, columns(orders)],
        out_specs=[columns(count) for count in parts],
        out_shape=[jax.ShapeDtypeStruct((count, rows), jnp.float32) for count in parts],
        cost_estimate=cost,
        name="fourier_second",
    )(*phases, high, low, came)


def legendre_kernel(
    sent, depth, last, parity_ref, zone_ref, tile_ref, place_ref, near_ref, came_ref, weights_ref, *rest
):
    folded = rest[-1]
    step = pl.program_id(0)
    count = near_ref.shape[0] // 2
    span = 2 * depth
    batch = near_ref.shape[1] // span
    width = weights_ref.shape[4]

    @pl.when(tile_ref[step] == 0)
    def _():
        total = near_ref[...] + came_ref[...]
        rows = total.reshape(2 * count, batch, span).astype(jnp.bfloat16)
        parity = lax.broadcasted_iota(jnp.int32, (2 * batch, span), 1) % 2
        for r in range(count):
            both = jnp.concatenate([rows[r], rows[count + r]], 0)
            zero = jnp.zeros_like(both)
            folded[r, : 2 * batch] = jnp.where(parity == 0, both, zero)
            folded[r, 2 * batch :] = jnp.where(parity == 1, both, zero)

    start = pl.multiple_of(place_ref[step], LANES)
    values = []
    for r in range(count):
        weights = weights_ref[0, r].reshape(span, width)
        value = jnp.dot(folded[r], weights, preferred_element_type=jnp.float32)
        values += [(r, e, value[e * 2 * batch : (e + 1) * 2 * batch]) for e in range(2)]
    if sent:
        for r, e, value in values:
            rest[0][r, e, :, pl.ds(start, width)] = value
        return
    add_ref, down_ref, up_ref = rest[:3]
    skip = add_ref.shape[3] - down_ref.shape[3]
    sums = [(r, e, value + add_ref[r, e, :, pl.ds(start, width)]) for r, e, value in values]

    @pl.when(zone_ref[step] < last)
    def _():
        for r, e, value in sums:
            down_ref[r, e, :, pl.ds(pl.multiple_of(start - skip, LANES), width)] = value

    @pl.when(zone_ref[step] > 0)
    def _():
        for r, e, value in sums:
            up_ref[r, e, :, pl.ds(start, width)] = value


def degree_plan(zones, half_degrees):
    widths = [-(-(half_degrees - half_degrees * z // zones) // LANES) * LANES for z in range(zones)]
    tile = min(2 * LANES, half_degrees)
    order = list(range(zones))[::-1]
    places, start = [0] * zones, 0
    for z in order:
        places[z] = start
        start += widths[z]
    steps = [(z, k, places[z] + k * tile) for z in order for k in range(-(-widths[z] // tile))]
    return widths, places, start, tile, np.array(steps, np.int32)


def project(plan, parity, place, count, own, near, came, weights, add=None):
    widths, places, total, tile, steps = plan
    zones = len(widths)
    depth = weights.shape[2]
    rows = near.shape[1]
    batch = rows // (2 * depth)
    first = 0 if add is not None else 1

    def rows_of(step, parity, zone, tile_, place_):
        return (first * zones + zone[step], 0)

    def weights_of(step, parity, zone, tile_, place_):
        return (0, (2 * zone[step] + parity[0]) * (own // count) + place // count, 0, 0, tile_[step])

    def lanes(width):
        return pl.BlockSpec((count, 2, 2 * batch, width), lambda step, *_: (0, 0, 0, 0))

    kept = [total - widths[-1], places[0] + tile - LANES]
    outs = [total] if add is None else kept
    in_specs = [
        pl.BlockSpec((2 * count, rows), rows_of),
        pl.BlockSpec((2 * count, rows), rows_of),
        pl.BlockSpec((1, count, depth, 2, tile), weights_of),
    ]
    operands = [near, came, weights]
    if add is not None:
        in_specs.append(lanes(total))
        operands.append(add)

    def kernel(*refs):
        legendre_kernel(add is None, depth, zones - 1, *refs)

    cells = len(steps) * count * tile
    return pl.pallas_call(
        kernel,
        grid_spec=pltpu.PrefetchScalarGridSpec(
            num_scalar_prefetch=4,
            grid=(len(steps),),
            in_specs=in_specs,
            out_specs=[lanes(width) for width in outs],
            scratch_shapes=[pltpu.VMEM((count, 4 * batch, 2 * depth), jnp.bfloat16)],
        ),
        out_shape=[
            jax.ShapeDtypeStruct((count, 2, 2 * batch, width), jnp.float32) for width in outs
        ],
        cost_estimate=pl.CostEstimate(
            flops=4 * cells * 4 * batch * depth,
            bytes_accessed=4 * cells * depth + 8 * count * batch * total,
            transcendentals=0,
        ),
        name="legendre_kept" if add is not None else "legendre_sent",
    )(parity.astype(jnp.int32).reshape(1), *[jnp.asarray(steps[:, k]) for k in range(3)], *operands)


def hop(value, source, target):
    pairs = [(2 * source + x, 2 * target + x) for x in range(2)]
    return lax.ppermute(value, "lat", pairs)


def after(value, *earlier):
    return lax.optimization_barrier((value, *earlier))[0]


def sizes(own):
    unit = own // 8
    if unit % 4:
        return [[own]]
    return [[unit * k for k in group] for group in SPLIT]


def local(grid, legendre):
    lon_count, lat_count = lax.axis_size("lon"), lax.axis_size("lat")
    lon, lat = lax.axis_index("lon"), lax.axis_index("lat")
    levels, longitudes = grid.shape[1], grid.shape[4]
    nlon = longitudes * lon_count
    per, half_degrees = legendre.shape[1], legendre.shape[4]
    own, zones = per // lat_count, lat_count // 2
    waves = per * lon_count
    side, zone = lat % 2, lat // 2
    plan = degree_plan(zones, half_degrees)
    widths, places, total = plan[:3]

    tendencies = folded_tendencies(grid)

    longitude = lon * longitudes + lax.iota(jnp.int32, longitudes)

    def table(wavenumbers, scale):
        product = wavenumbers[..., None] * longitude % nlon
        angles = product.astype(jnp.float32) * (2.0 * math.pi / nlon)
        return jnp.cos(angles) * scale, jnp.sin(angles) * scale

    bands = jnp.stack([2 * lax.iota(jnp.int32, zones) + (side ^ k) for k in range(2)], 0)
    coarse = table(lon_count * own * bands.reshape(-1), 1.0)
    keep = list(range(lon_count - 2, -1, -2))
    halves = [keep[: len(keep) // 2], keep[len(keep) // 2 :]]

    def phases(bit, chunks):
        blocks = []
        for rels in halves:
            for place, count in chunks:
                fine = lon_count * (place + lax.iota(jnp.int32, count))
                fine = jnp.stack([lon ^ (rel | bit) for rel in rels])[:, None] + fine
                cos, sin = table(fine, 1.0 / math.sqrt(nlon))
                first = jnp.concatenate([cos, -sin], 1)[:, None]
                second = jnp.concatenate([sin, cos], 1)[:, None]
                both = coarse[0][:, None] * first - coarse[1][:, None] * second
                blocks.append(both.reshape(-1, longitudes))
        both = jnp.concatenate(blocks, 0)
        top = lax.reduce_precision(both, 8, 7)
        return top.astype(jnp.bfloat16), (both - top).astype(jnp.bfloat16)

    def lon_swap(value, bit):
        return lax.ppermute(value, "lon", [(i, i ^ bit) for i in range(lon_count)])

    groups, place = [], 0
    for group in sizes(own):
        chunks = []
        for count in group:
            chunks.append((place, count))
            place += count
        groups.append(chunks)

    swapped, before = [], None
    for chunks in groups:
        here = tendencies if before is None else (after(tendencies[0], before), tendencies[1])
        ready = phases(1, chunks)
        before = fourier(ready, here)
        swapped.append(lon_swap(before, 1))
    pieces = []
    for chunks, came in zip(groups, swapped):
        parts = [len(keep) // 2 * 4 * zones * count for _, count in chunks] * 2
        here = (after(tendencies[0], before), tendencies[1])
        ready = phases(0, chunks)
        blocks = fourier(ready, here, came, parts)
        before = blocks[-1]
        for k, (place, count) in enumerate(chunks):
            far, near = blocks[k], blocks[len(chunks) + k]
            bit = lon_count // 2
            while bit > 2:
                near = near + lon_swap(far, bit)
                rows = near.shape[0] // 2
                far, near = near[:rows], near[rows:]
                bit //= 2
            pieces.append((place, count, near, lon_swap(far, bit)))

    def finish(count, place, mine):
        mine = mine.reshape(count, 2, 2, 8, levels, half_degrees).transpose(0, 3, 4, 2, 1, 5)
        wavenumber = lon + lon_count * (lat * own + place + lax.iota(jnp.int32, count))
        degree = (
            2 * lax.iota(jnp.int32, half_degrees)[None, None, :]
            + lax.iota(jnp.int32, 2)[None, :, None]
        )
        inside = wavenumber[:, None, None] + degree < waves
        return jnp.where(inside[:, None, None, None, :, :], mine, jnp.zeros((), jnp.float32))

    result = jnp.zeros((own, 8, levels, 2, 2, half_degrees), jnp.float32)
    given, chains, states, kept = [None] * len(pieces), [], [], []

    def send(k):
        place, count, near, came = pieces[k]
        if k > 1:
            near = after(near, *kept[k - 2])
        (value,) = project(plan, 1 - side, place, count, own, near, came, legendre)
        given[k] = lax.ppermute(value, "lat", [(i, i ^ 1) for i in range(lat_count)])

    for k, (place, count, near, came) in enumerate(pieces):
        if k == 0:
            send(0)
        if k + 1 < len(pieces):
            send(k + 1)
        waits = []
        for number, chain in enumerate(chains):
            state = next(chain, None)
            if state is not None:
                states[number] = state
                waits.extend(state)
        near = after(near, *waits) if waits else near
        block = project(plan, side, place, count, own, near, came, legendre, given[k])
        kept.append(block)
        chains.append(line(block, zones, zone, plan, half_degrees))
        states.append(next(chains[-1]))
    for k, chain in enumerate(chains):
        for state in chain:
            states[k] = state
        place, count = pieces[k][:2]
        mine = finish(count, place, states[k][0])
        result = lax.dynamic_update_slice(result, mine, (place,) + (0,) * 5)
    return result[None]


def line(block, zones, zone, plan, half_degrees):
    widths, places, _ = plan[:3]
    downs, ups = [block[0]], [block[1]]
    came_down, came_up = [], []
    for k in range(zones - 1):
        came_down.append(hop(downs[k], zones - 1 - k, zones - 2 - k))
        came_up.append(hop(ups[k], k, k + 1))
        yield (downs[k], ups[k])
        if k < zones - 2:
            cut = widths[zones - 2 - k]
            downs.append(downs[k][..., cut:] + came_down[k][..., cut:])
            ups.append(ups[k][..., : places[k + 1]] + came_up[k][..., : places[k + 1]])
    downs, ups, came_down, came_up = lax.optimization_barrier((downs, ups, came_down, came_up))
    mine = None
    for z in range(zones):
        width = widths[z]
        if z == zones - 1:
            value = ups[0][..., :width]
        else:
            k = zones - 2 - z
            value = downs[k][..., :width] + came_down[k][..., :width]
        if z > 0:
            value = value + came_up[z - 1][..., places[z] : places[z] + width]
        value = jnp.pad(value, ((0, 0), (0, 0), (0, 0), (0, half_degrees - width)))
        mine = value if mine is None else jnp.where(zone == z, value, mine)
    yield (mine,)


def solution(mesh):
    in_specs = (P(None, None, None, "lat", "lon"), P("lon", None, "lat", None, None))
    out_specs = P("lon", "lat", None, None, None, None, None)

    return jax.shard_map(local, mesh=mesh, in_specs=in_specs, out_specs=out_specs, check_vma=False)
```

```python
import math

import jax
import jax.numpy as jnp
import numpy as np
from jax import lax
from jax.experimental import pallas as pl
from jax.experimental.pallas import tpu as pltpu
from jax.sharding import PartitionSpec as P


ADIABATIC = 0.286
LANES = 128
SPLIT = ((1, 1, 2), (2, 1, 1))
ROWS_CONTRACTED = (((1,), (1,)), ((), ()))


def tendency_kernel(grid_ref, high_ref, low_ref, scratch):
    pairs = grid_ref.shape[3]
    pieces = grid_ref.shape[4] // LANES

    def field(n):
        return [grid_ref[n, 0, h].astype(jnp.float32) for h in range(2)]

    u, v, zeta, div, temp, hum, temp_x, temp_y, hum_x, hum_y, press_x, press_y = [
        field(n) for n in range(12)
    ]
    formulas = [
        lambda h: zeta[h] * v[h] - temp[h] * press_x[h],
        lambda h: -zeta[h] * u[h] - temp[h] * press_y[h],
        lambda h: u[h] * v[h],
        lambda h: -(u[h] * temp_x[h] + v[h] * temp_y[h]) + ADIABATIC * temp[h] * div[h],
        lambda h: -(u[h] * hum_x[h] + v[h] * hum_y[h]) - hum[h] * div[h],
        lambda h: u[h] * temp[h],
        lambda h: v[h] * temp[h],
        lambda h: v[h] * hum[h],
    ]
    for t, formula in enumerate(formulas):
        north, south = formula(0), formula(1)
        even, odd = north + south, north - south
        for piece in range(pieces):
            lanes = slice(piece * LANES, (piece + 1) * LANES)
            place = t * pieces + piece
            scratch[place, pl.ds(0, pairs, stride=2), :] = even[:, lanes]
            scratch[place, pl.ds(1, pairs, stride=2), :] = odd[:, lanes]
            whole = scratch[place]
            high = whole.astype(jnp.bfloat16)
            high_ref[t, 0, :, lanes] = high
            low_ref[t, 0, :, lanes] = (whole - high.astype(jnp.float32)).astype(jnp.bfloat16)


def folded_tendencies(grid):
    fields, levels, hemispheres, pairs, longitudes = grid.shape
    width = min(256, longitudes)
    shape = jax.ShapeDtypeStruct((8, levels, 2 * pairs, longitudes), jnp.bfloat16)
    high, low = pl.pallas_call(
        tendency_kernel,
        grid=(levels, longitudes // width),
        in_specs=[
            pl.BlockSpec((fields, 1, hemispheres, pairs, width), lambda l, x: (0, l, 0, 0, x))
        ],
        out_specs=[pl.BlockSpec((8, 1, 2 * pairs, width), lambda l, x: (0, l, 0, x))] * 2,
        out_shape=(shape, shape),
        scratch_shapes=[pltpu.VMEM((8 * width // LANES, 2 * pairs, LANES), jnp.float32)],
        cost_estimate=pl.CostEstimate(
            flops=4 * grid.size, bytes_accessed=5 * grid.size, transcendentals=0
        ),
        name="tendencies",
    )(grid)
    rows = 8 * levels * 2 * pairs
    return high.reshape(rows, longitudes), low.reshape(rows, longitudes)


def product3(phase_high, phase_low, high, low):
    def one(a, b):
        return lax.dot_general(a, b, ROWS_CONTRACTED, preferred_element_type=jnp.float32)

    return one(phase_high, high) + (one(phase_high, low) + one(phase_low, high))


def first_fourier_kernel(ph_ref, pl_ref, high_ref, low_ref, out_ref):
    out_ref[...] = product3(ph_ref[...], pl_ref[...], high_ref[...], low_ref[...])


def second_fourier_kernel(ph_ref, pl_ref, high_ref, low_ref, came_ref, *out_refs):
    total = product3(ph_ref[...], pl_ref[...], high_ref[...], low_ref[...]) + came_ref[...]
    start = 0
    for out_ref in out_refs:
        rows = out_ref.shape[0]
        out_ref[...] = total[start : start + rows]
        start += rows


def fourier(phases, tendencies, came=None, parts=()):
    high, low = tendencies
    orders, longitudes = phases[0].shape
    rows = high.shape[0]
    block = min(512, rows)
    whole = pl.BlockSpec((orders, longitudes), lambda r: (0, 0))
    part = pl.BlockSpec((block, longitudes), lambda r: (r, 0))

    def columns(count):
        return pl.BlockSpec((count, block), lambda r: (0, r))

    cost = pl.CostEstimate(
        flops=6 * orders * longitudes * rows,
        bytes_accessed=4 * rows * (longitudes + orders),
        transcendentals=0,
    )
    if came is None:
        return pl.pallas_call(
            first_fourier_kernel,
            grid=(rows // block,),
            in_specs=[whole, whole, part, part],
            out_specs=columns(orders),
            out_shape=jax.ShapeDtypeStruct((orders, rows), jnp.float32),
            cost_estimate=cost,
            name="fourier_first",
        )(*phases, high, low)
    return pl.pallas_call(
        second_fourier_kernel,
        grid=(rows // block,),
        in_specs=[whole, whole, part, part, columns(orders)],
        out_specs=[columns(count) for count in parts],
        out_shape=[jax.ShapeDtypeStruct((count, rows), jnp.float32) for count in parts],
        cost_estimate=cost,
        name="fourier_second",
    )(*phases, high, low, came)


def legendre_kernel(
    sent, depth, last, parity_ref, zone_ref, tile_ref, place_ref, near_ref, came_ref, weights_ref, *rest
):
    folded = rest[-1]
    step = pl.program_id(0)
    count = near_ref.shape[0] // 2
    span = 2 * depth
    batch = near_ref.shape[1] // span
    width = weights_ref.shape[4]

    @pl.when(tile_ref[step] == 0)
    def _():
        total = near_ref[...] + came_ref[...]
        rows = total.reshape(2 * count, batch, span).astype(jnp.bfloat16)
        parity = lax.broadcasted_iota(jnp.int32, (2 * batch, span), 1) % 2
        for r in range(count):
            both = jnp.concatenate([rows[r], rows[count + r]], 0)
            zero = jnp.zeros_like(both)
            folded[r, : 2 * batch] = jnp.where(parity == 0, both, zero)
            folded[r, 2 * batch :] = jnp.where(parity == 1, both, zero)

    start = pl.multiple_of(place_ref[step], LANES)
    values = []
    for r in range(count):
        weights = weights_ref[0, r].reshape(span, width)
        value = jnp.dot(folded[r], weights, preferred_element_type=jnp.float32)
        values += [(r, e, value[e * 2 * batch : (e + 1) * 2 * batch]) for e in range(2)]
    if sent:
        for r, e, value in values:
            rest[0][r, e, :, pl.ds(start, width)] = value
        return
    add_ref, down_ref, up_ref = rest[:3]
    skip = add_ref.shape[3] - down_ref.shape[3]
    sums = [(r, e, value + add_ref[r, e, :, pl.ds(start, width)]) for r, e, value in values]

    @pl.when(zone_ref[step] < last)
    def _():
        for r, e, value in sums:
            down_ref[r, e, :, pl.ds(pl.multiple_of(start - skip, LANES), width)] = value

    @pl.when(zone_ref[step] > 0)
    def _():
        for r, e, value in sums:
            up_ref[r, e, :, pl.ds(start, width)] = value


def degree_plan(zones, half_degrees):
    widths = [-(-(half_degrees - half_degrees * z // zones) // LANES) * LANES for z in range(zones)]
    tile = min(2 * LANES, half_degrees)
    order = list(range(zones))[::-1]
    places, start = [0] * zones, 0
    for z in order:
        places[z] = start
        start += widths[z]
    steps = [(z, k, places[z] + k * tile) for z in order for k in range(-(-widths[z] // tile))]
    return widths, places, start, tile, np.array(steps, np.int32)


def project(plan, parity, place, count, own, near, came, weights, add=None):
    widths, places, total, tile, steps = plan
    zones = len(widths)
    depth = weights.shape[2]
    rows = near.shape[1]
    batch = rows // (2 * depth)
    first = 0 if add is not None else 1

    def rows_of(step, parity, zone, tile_, place_):
        return (first * zones + zone[step], 0)

    def weights_of(step, parity, zone, tile_, place_):
        return (0, (2 * zone[step] + parity[0]) * (own // count) + place // count, 0, 0, tile_[step])

    def lanes(width):
        return pl.BlockSpec((count, 2, 2 * batch, width), lambda step, *_: (0, 0, 0, 0))

    kept = [total - widths[-1], places[0] + tile - LANES]
    outs = [total] if add is None else kept
    in_specs = [
        pl.BlockSpec((2 * count, rows), rows_of),
        pl.BlockSpec((2 * count, rows), rows_of),
        pl.BlockSpec((1, count, depth, 2, tile), weights_of),
    ]
    operands = [near, came, weights]
    if add is not None:
        in_specs.append(lanes(total))
        operands.append(add)

    def kernel(*refs):
        legendre_kernel(add is None, depth, zones - 1, *refs)

    cells = len(steps) * count * tile
    return pl.pallas_call(
        kernel,
        grid_spec=pltpu.PrefetchScalarGridSpec(
            num_scalar_prefetch=4,
            grid=(len(steps),),
            in_specs=in_specs,
            out_specs=[lanes(width) for width in outs],
            scratch_shapes=[pltpu.VMEM((count, 4 * batch, 2 * depth), jnp.bfloat16)],
        ),
        out_shape=[
            jax.ShapeDtypeStruct((count, 2, 2 * batch, width), jnp.float32) for width in outs
        ],
        cost_estimate=pl.CostEstimate(
            flops=4 * cells * 4 * batch * depth,
            bytes_accessed=4 * cells * depth + 8 * count * batch * total,
            transcendentals=0,
        ),
        name="legendre_kept" if add is not None else "legendre_sent",
    )(parity.astype(jnp.int32).reshape(1), *[jnp.asarray(steps[:, k]) for k in range(3)], *operands)


def hop(value, source, target):
    pairs = [(2 * source + x, 2 * target + x) for x in range(2)]
    return lax.ppermute(value, "lat", pairs)


def after(value, *earlier):
    return lax.optimization_barrier((value, *earlier))[0]


def sizes(own):
    unit = own // 8
    if unit % 4:
        return [[own]]
    return [[unit * k for k in group] for group in SPLIT]


def local(grid, legendre):
    lon_count, lat_count = lax.axis_size("lon"), lax.axis_size("lat")
    lon, lat = lax.axis_index("lon"), lax.axis_index("lat")
    levels, longitudes = grid.shape[1], grid.shape[4]
    nlon = longitudes * lon_count
    per, half_degrees = legendre.shape[1], legendre.shape[4]
    own, zones = per // lat_count, lat_count // 2
    waves = per * lon_count
    side, zone = lat % 2, lat // 2
    plan = degree_plan(zones, half_degrees)
    widths, places, total = plan[:3]

    tendencies = folded_tendencies(grid)

    longitude = lon * longitudes + lax.iota(jnp.int32, longitudes)

    def table(wavenumbers, scale):
        product = wavenumbers[..., None] * longitude % nlon
        angles = product.astype(jnp.float32) * (2.0 * math.pi / nlon)
        return jnp.cos(angles) * scale, jnp.sin(angles) * scale

    bands = jnp.stack([2 * lax.iota(jnp.int32, zones) + (side ^ k) for k in range(2)], 0)
    coarse = table(lon_count * own * bands.reshape(-1), 1.0)
    keep = list(range(lon_count - 2, -1, -2))
    halves = [keep[: len(keep) // 2], keep[len(keep) // 2 :]]

    steps = lon_count * lax.iota(jnp.int32, own)
    rels = jnp.stack([lon ^ rel for rel in range(lon_count)])
    cos, sin = table(rels[:, None] + steps, 1.0 / math.sqrt(nlon))

    def phases(bit, chunks):
        blocks = []
        for some in halves:
            for place, count in chunks:
                def fine(values):
                    return jnp.stack([values[rel | bit, place : place + count] for rel in some])

                first = jnp.concatenate([fine(cos), -fine(sin)], 1)[:, None]
                second = jnp.concatenate([fine(sin), fine(cos)], 1)[:, None]
                both = coarse[0][:, None] * first - coarse[1][:, None] * second
                blocks.append(both.reshape(-1, longitudes))
        both = jnp.concatenate(blocks, 0)
        top = lax.reduce_precision(both, 8, 7)
        return top.astype(jnp.bfloat16), (both - top).astype(jnp.bfloat16)

    def lon_swap(value, bit):
        return lax.ppermute(value, "lon", [(i, i ^ bit) for i in range(lon_count)])

    groups, place = [], 0
    for group in sizes(own):
        chunks = []
        for count in group:
            chunks.append((place, count))
            place += count
        groups.append(chunks)

    swapped, before = [], None
    for chunks in groups:
        here = tendencies if before is None else (after(tendencies[0], before), tendencies[1])
        ready = phases(1, chunks)
        before = fourier(ready, here)
        swapped.append(lon_swap(before, 1))
    pieces = []
    for chunks, came in zip(groups, swapped):
        parts = [len(keep) // 2 * 4 * zones * count for _, count in chunks] * 2
        here = (after(tendencies[0], before), tendencies[1])
        ready = phases(0, chunks)
        blocks = fourier(ready, here, came, parts)
        before = blocks[-1]
        for k, (place, count) in enumerate(chunks):
            far, near = blocks[k], blocks[len(chunks) + k]
            bit = lon_count // 2
            while bit > 2:
                near = near + lon_swap(far, bit)
                rows = near.shape[0] // 2
                far, near = near[:rows], near[rows:]
                bit //= 2
            pieces.append((place, count, near, lon_swap(far, bit)))

    def finish(count, place, mine):
        mine = mine.reshape(count, 2, 2, 8, levels, half_degrees).transpose(0, 3, 4, 2, 1, 5)
        wavenumber = lon + lon_count * (lat * own + place + lax.iota(jnp.int32, count))
        degree = (
            2 * lax.iota(jnp.int32, half_degrees)[None, None, :]
            + lax.iota(jnp.int32, 2)[None, :, None]
        )
        inside = wavenumber[:, None, None] + degree < waves
        return jnp.where(inside[:, None, None, None, :, :], mine, jnp.zeros((), jnp.float32))

    result = jnp.zeros((own, 8, levels, 2, 2, half_degrees), jnp.float32)
    given, chains, kept = [None] * len(pieces), [], []

    def send(k):
        place, count, near, came = pieces[k]
        if k > 1:
            near = after(near, *kept[k - 2])
        (value,) = project(plan, 1 - side, place, count, own, near, came, legendre)
        given[k] = lax.ppermute(value, "lat", [(i, i ^ 1) for i in range(lat_count)])

    rounds = max(zones - 1, 1)
    for k, (place, count, near, came) in enumerate(pieces):
        if k == 0:
            send(0)
        if k + 1 < len(pieces):
            send(k + 1)
        waits = []
        for number, chain in enumerate(chains):
            if k - number < rounds:
                waits.extend(next(chain))
        near = after(near, *waits) if waits else near
        block = project(plan, side, place, count, own, near, came, legendre, given[k])
        kept.append(block)
        chains.append(line(block, zones, plan))
        next(chains[-1])
    ends = []
    for chain in chains:
        state = None
        for state in chain:
            pass
        ends.append(state)
    parts = []
    for numbers in (range(len(ends) - 1), range(len(ends) - 1, len(ends))):
        if len(numbers) == 0:
            continue
        blocks = [close(*ends[k], zone, plan, half_degrees, kept[-1]) for k in numbers]
        place = pieces[numbers[0]][0]
        count = sum(pieces[k][1] for k in numbers)
        mine = finish(count, place, jnp.concatenate(blocks, 0))
        result = lax.dynamic_update_slice(result, mine, (place,) + (0,) * 5)
        parts.append(mine)
    return result[None]


def line(block, zones, plan):
    widths, places, _ = plan[:3]
    downs, ups = [block[0]], [block[1]]
    came_down, came_up = [], []
    for k in range(zones - 1):
        came_down.append(hop(downs[k], zones - 1 - k, zones - 2 - k))
        came_up.append(hop(ups[k], k, k + 1))
        yield (downs[k], ups[k])
        if k < zones - 2:
            cut = widths[zones - 2 - k]
            downs.append(downs[k][..., cut:] + came_down[k][..., cut:])
            ups.append(ups[k][..., : places[k + 1]] + came_up[k][..., : places[k + 1]])
    yield downs, ups, came_down, came_up


def close(downs, ups, came_down, came_up, zone, plan, half_degrees, last):
    widths, places, _ = plan[:3]
    zones = len(widths)
    downs, ups, came_down, came_up, _ = lax.optimization_barrier(
        (downs, ups, came_down, came_up, last)
    )
    mine = None
    for z in range(zones):
        width = widths[z]
        if z == zones - 1:
            value = ups[0][..., :width]
        else:
            k = zones - 2 - z
            value = downs[k][..., :width] + came_down[k][..., :width]
        if z > 0:
            value = value + came_up[z - 1][..., places[z] : places[z] + width]
        value = jnp.pad(value, ((0, 0), (0, 0), (0, 0), (0, half_degrees - width)))
        mine = value if mine is None else jnp.where(zone == z, value, mine)
    return mine


def solution(mesh):
    in_specs = (P(None, None, None, "lat", "lon"), P("lon", None, "lat", None, None))
    out_specs = P("lon", "lat", None, None, None, None, None)

    return jax.shard_map(local, mesh=mesh, in_specs=in_specs, out_specs=out_specs, check_vma=False)
```

```python
import math

import jax
import jax.numpy as jnp
import numpy as np
from jax import lax
from jax.experimental import pallas as pl
from jax.experimental.pallas import tpu as pltpu
from jax.sharding import PartitionSpec as P


ADIABATIC = 0.286
LANES = 128
SPLIT = ((1, 1, 2), (2, 1, 1))
ROWS_CONTRACTED = (((1,), (1,)), ((), ()))


def tendency_kernel(grid_ref, high_ref, low_ref, scratch):
    pairs = grid_ref.shape[3]
    pieces = grid_ref.shape[4] // LANES

    def field(n):
        return [grid_ref[n, 0, h].astype(jnp.float32) for h in range(2)]

    u, v, zeta, div, temp, hum, temp_x, temp_y, hum_x, hum_y, press_x, press_y = [
        field(n) for n in range(12)
    ]
    formulas = [
        lambda h: zeta[h] * v[h] - temp[h] * press_x[h],
        lambda h: -zeta[h] * u[h] - temp[h] * press_y[h],
        lambda h: u[h] * v[h],
        lambda h: -(u[h] * temp_x[h] + v[h] * temp_y[h]) + ADIABATIC * temp[h] * div[h],
        lambda h: -(u[h] * hum_x[h] + v[h] * hum_y[h]) - hum[h] * div[h],
        lambda h: u[h] * temp[h],
        lambda h: v[h] * temp[h],
        lambda h: v[h] * hum[h],
    ]
    for t, formula in enumerate(formulas):
        north, south = formula(0), formula(1)
        even, odd = north + south, north - south
        for piece in range(pieces):
            lanes = slice(piece * LANES, (piece + 1) * LANES)
            place = t * pieces + piece
            scratch[place, pl.ds(0, pairs, stride=2), :] = even[:, lanes]
            scratch[place, pl.ds(1, pairs, stride=2), :] = odd[:, lanes]
            whole = scratch[place]
            high = whole.astype(jnp.bfloat16)
            high_ref[t, 0, :, lanes] = high
            low_ref[t, 0, :, lanes] = (whole - high.astype(jnp.float32)).astype(jnp.bfloat16)


def folded_tendencies(grid):
    fields, levels, hemispheres, pairs, longitudes = grid.shape
    width = min(256, longitudes)
    shape = jax.ShapeDtypeStruct((8, levels, 2 * pairs, longitudes), jnp.bfloat16)
    high, low = pl.pallas_call(
        tendency_kernel,
        grid=(levels, longitudes // width),
        in_specs=[
            pl.BlockSpec((fields, 1, hemispheres, pairs, width), lambda l, x: (0, l, 0, 0, x))
        ],
        out_specs=[pl.BlockSpec((8, 1, 2 * pairs, width), lambda l, x: (0, l, 0, x))] * 2,
        out_shape=(shape, shape),
        scratch_shapes=[pltpu.VMEM((8 * width // LANES, 2 * pairs, LANES), jnp.float32)],
        cost_estimate=pl.CostEstimate(
            flops=4 * grid.size, bytes_accessed=5 * grid.size, transcendentals=0
        ),
        name="tendencies",
    )(grid)
    rows = 8 * levels * 2 * pairs
    return high.reshape(rows, longitudes), low.reshape(rows, longitudes)


def product3(phase_high, phase_low, high, low):
    def one(a, b):
        return lax.dot_general(a, b, ROWS_CONTRACTED, preferred_element_type=jnp.float32)

    return one(phase_high, high) + (one(phase_high, low) + one(phase_low, high))


def first_fourier_kernel(ph_ref, pl_ref, high_ref, low_ref, out_ref):
    out_ref[...] = product3(ph_ref[...], pl_ref[...], high_ref[...], low_ref[...])


def second_fourier_kernel(ph_ref, pl_ref, high_ref, low_ref, came_ref, *out_refs):
    total = product3(ph_ref[...], pl_ref[...], high_ref[...], low_ref[...]) + came_ref[...]
    start = 0
    for out_ref in out_refs:
        rows = out_ref.shape[0]
        out_ref[...] = total[start : start + rows]
        start += rows


def fourier(phases, tendencies, came=None, parts=()):
    high, low = tendencies
    orders, longitudes = phases[0].shape
    rows = high.shape[0]
    block = min(512, rows)
    whole = pl.BlockSpec((orders, longitudes), lambda r: (0, 0))
    part = pl.BlockSpec((block, longitudes), lambda r: (r, 0))

    def columns(count):
        return pl.BlockSpec((count, block), lambda r: (0, r))

    cost = pl.CostEstimate(
        flops=6 * orders * longitudes * rows,
        bytes_accessed=4 * rows * (longitudes + orders),
        transcendentals=0,
    )
    if came is None:
        return pl.pallas_call(
            first_fourier_kernel,
            grid=(rows // block,),
            in_specs=[whole, whole, part, part],
            out_specs=columns(orders),
            out_shape=jax.ShapeDtypeStruct((orders, rows), jnp.float32),
            cost_estimate=cost,
            name="fourier_first",
        )(*phases, high, low)
    return pl.pallas_call(
        second_fourier_kernel,
        grid=(rows // block,),
        in_specs=[whole, whole, part, part, columns(orders)],
        out_specs=[columns(count) for count in parts],
        out_shape=[jax.ShapeDtypeStruct((count, rows), jnp.float32) for count in parts],
        cost_estimate=cost,
        name="fourier_second",
    )(*phases, high, low, came)


def legendre_kernel(
    sent, depth, last, parity_ref, zone_ref, tile_ref, place_ref, near_ref, came_ref, weights_ref, *rest
):
    folded = rest[-1]
    step = pl.program_id(0)
    count = near_ref.shape[0] // 2
    span = 2 * depth
    batch = near_ref.shape[1] // span
    width = weights_ref.shape[4]

    @pl.when(tile_ref[step] == 0)
    def _():
        total = near_ref[...] + came_ref[...]
        rows = total.reshape(2 * count, batch, span).astype(jnp.bfloat16)
        parity = lax.broadcasted_iota(jnp.int32, (2 * batch, span), 1) % 2
        for r in range(count):
            both = jnp.concatenate([rows[r], rows[count + r]], 0)
            zero = jnp.zeros_like(both)
            folded[r, : 2 * batch] = jnp.where(parity == 0, both, zero)
            folded[r, 2 * batch :] = jnp.where(parity == 1, both, zero)

    start = pl.multiple_of(place_ref[step], LANES)
    values = []
    for r in range(count):
        weights = weights_ref[0, r].reshape(span, width)
        value = jnp.dot(folded[r], weights, preferred_element_type=jnp.float32)
        values += [(r, e, value[e * 2 * batch : (e + 1) * 2 * batch]) for e in range(2)]
    if sent:
        for r, e, value in values:
            rest[0][r, e, :, pl.ds(start, width)] = value
        return
    add_ref, down_ref, up_ref = rest[:3]
    skip = add_ref.shape[3] - down_ref.shape[3]
    sums = [(r, e, value + add_ref[r, e, :, pl.ds(start, width)]) for r, e, value in values]

    @pl.when(zone_ref[step] < last)
    def _():
        for r, e, value in sums:
            down_ref[r, e, :, pl.ds(pl.multiple_of(start - skip, LANES), width)] = value

    @pl.when(zone_ref[step] > 0)
    def _():
        for r, e, value in sums:
            up_ref[r, e, :, pl.ds(start, width)] = value


def degree_plan(zones, half_degrees):
    widths = [-(-(half_degrees - half_degrees * z // zones) // LANES) * LANES for z in range(zones)]
    tile = min(2 * LANES, half_degrees)
    order = list(range(zones))[::-1]
    places, start = [0] * zones, 0
    for z in order:
        places[z] = start
        start += widths[z]
    steps = [(z, k, places[z] + k * tile) for z in order for k in range(-(-widths[z] // tile))]
    return widths, places, start, tile, np.array(steps, np.int32)


def project(plan, parity, place, count, own, near, came, weights, add=None):
    widths, places, total, tile, steps = plan
    zones = len(widths)
    depth = weights.shape[2]
    rows = near.shape[1]
    batch = rows // (2 * depth)
    first = 0 if add is not None else 1

    def rows_of(step, parity, zone, tile_, place_):
        return (first * zones + zone[step], 0)

    def weights_of(step, parity, zone, tile_, place_):
        return (0, (2 * zone[step] + parity[0]) * (own // count) + place // count, 0, 0, tile_[step])

    def lanes(width):
        return pl.BlockSpec((count, 2, 2 * batch, width), lambda step, *_: (0, 0, 0, 0))

    kept = [total - widths[-1], places[0] + tile - LANES]
    outs = [total] if add is None else kept
    in_specs = [
        pl.BlockSpec((2 * count, rows), rows_of),
        pl.BlockSpec((2 * count, rows), rows_of),
        pl.BlockSpec((1, count, depth, 2, tile), weights_of),
    ]
    operands = [near, came, weights]
    if add is not None:
        in_specs.append(lanes(total))
        operands.append(add)

    def kernel(*refs):
        legendre_kernel(add is None, depth, zones - 1, *refs)

    cells = len(steps) * count * tile
    return pl.pallas_call(
        kernel,
        grid_spec=pltpu.PrefetchScalarGridSpec(
            num_scalar_prefetch=4,
            grid=(len(steps),),
            in_specs=in_specs,
            out_specs=[lanes(width) for width in outs],
            scratch_shapes=[pltpu.VMEM((count, 4 * batch, 2 * depth), jnp.bfloat16)],
        ),
        out_shape=[
            jax.ShapeDtypeStruct((count, 2, 2 * batch, width), jnp.float32) for width in outs
        ],
        cost_estimate=pl.CostEstimate(
            flops=4 * cells * 4 * batch * depth,
            bytes_accessed=4 * cells * depth + 8 * count * batch * total,
            transcendentals=0,
        ),
        name="legendre_kept" if add is not None else "legendre_sent",
    )(parity.astype(jnp.int32).reshape(1), *[jnp.asarray(steps[:, k]) for k in range(3)], *operands)


def hop(value, source, target):
    pairs = [(2 * source + x, 2 * target + x) for x in range(2)]
    return lax.ppermute(value, "lat", pairs)


def after(value, *earlier):
    return lax.optimization_barrier((value, *earlier))[0]


def sizes(own):
    unit = own // 8
    if unit % 4:
        return [[own]]
    return [[unit * k for k in group] for group in SPLIT]


def local(grid, legendre):
    lon_count, lat_count = lax.axis_size("lon"), lax.axis_size("lat")
    lon, lat = lax.axis_index("lon"), lax.axis_index("lat")
    levels, longitudes = grid.shape[1], grid.shape[4]
    nlon = longitudes * lon_count
    per, half_degrees = legendre.shape[1], legendre.shape[4]
    own, zones = per // lat_count, lat_count // 2
    waves = per * lon_count
    side, zone = lat % 2, lat // 2
    plan = degree_plan(zones, half_degrees)
    widths, places, total = plan[:3]

    tendencies = folded_tendencies(grid)

    longitude = lon * longitudes + lax.iota(jnp.int32, longitudes)

    def table(wavenumbers, scale):
        product = wavenumbers[..., None] * longitude % nlon
        angles = product.astype(jnp.float32) * (2.0 * math.pi / nlon)
        return jnp.cos(angles) * scale, jnp.sin(angles) * scale

    bands = jnp.stack([2 * lax.iota(jnp.int32, zones) + (side ^ k) for k in range(2)], 0)
    coarse = table(lon_count * own * bands.reshape(-1), 1.0)
    keep = list(range(lon_count - 2, -1, -2))
    halves = [keep[: len(keep) // 2], keep[len(keep) // 2 :]]

    steps = lon_count * lax.iota(jnp.int32, own)
    rels = jnp.stack([lon ^ rel for rel in range(lon_count)])
    cos, sin = table(rels[:, None] + steps, 1.0 / math.sqrt(nlon))

    def phases(bit, chunks):
        blocks = []
        for some in halves:
            for place, count in chunks:
                def fine(values):
                    return jnp.stack([values[rel | bit, place : place + count] for rel in some])

                first = jnp.concatenate([fine(cos), -fine(sin)], 1)[:, None]
                second = jnp.concatenate([fine(sin), fine(cos)], 1)[:, None]
                both = coarse[0][:, None] * first - coarse[1][:, None] * second
                blocks.append(both.reshape(-1, longitudes))
        both = jnp.concatenate(blocks, 0)
        top = lax.reduce_precision(both, 8, 7)
        return top.astype(jnp.bfloat16), (both - top).astype(jnp.bfloat16)

    def lon_swap(value, bit):
        return lax.ppermute(value, "lon", [(i, i ^ bit) for i in range(lon_count)])

    groups, place = [], 0
    for group in sizes(own):
        chunks = []
        for count in group:
            chunks.append((place, count))
            place += count
        groups.append(chunks)

    swapped, before = [], None
    for chunks in groups:
        here = tendencies if before is None else (after(tendencies[0], before), tendencies[1])
        ready = phases(1, chunks)
        before = fourier(ready, here)
        swapped.append(lon_swap(before, 1))
    pieces = []
    for chunks, came in zip(groups, swapped):
        parts = [len(keep) // 2 * 4 * zones * count for _, count in chunks] * 2
        here = (after(tendencies[0], before), tendencies[1])
        ready = phases(0, chunks)
        blocks = fourier(ready, here, came, parts)
        before = blocks[-1]
        for k, (place, count) in enumerate(chunks):
            far, near = blocks[k], blocks[len(chunks) + k]
            bit = lon_count // 2
            while bit > 2:
                near = near + lon_swap(far, bit)
                rows = near.shape[0] // 2
                far, near = near[:rows], near[rows:]
                bit //= 2
            pieces.append((place, count, near, lon_swap(far, bit)))

    def finish(count, place, mine):
        mine = mine.reshape(count, 2, 2, 8, levels, half_degrees).transpose(0, 3, 4, 2, 1, 5)
        wavenumber = lon + lon_count * (lat * own + place + lax.iota(jnp.int32, count))
        degree = (
            2 * lax.iota(jnp.int32, half_degrees)[None, None, :]
            + lax.iota(jnp.int32, 2)[None, :, None]
        )
        inside = wavenumber[:, None, None] + degree < waves
        return jnp.where(inside[:, None, None, None, :, :], mine, jnp.zeros((), jnp.float32))

    result = jnp.zeros((own, 8, levels, 2, 2, half_degrees), jnp.float32)
    given, chains, kept = [None] * len(pieces), [], []

    def send(k):
        place, count, near, came = pieces[k]
        if k > 1:
            near = after(near, *kept[k - 2])
        (value,) = project(plan, 1 - side, place, count, own, near, came, legendre)
        given[k] = lax.ppermute(value, "lat", [(i, i ^ 1) for i in range(lat_count)])

    rounds = max(zones - 1, 1)
    for k, (place, count, near, came) in enumerate(pieces):
        if k == 0:
            send(0)
        if k + 1 < len(pieces):
            send(k + 1)
        waits = []
        for number, chain in enumerate(chains):
            if 2 <= k - number <= rounds:
                waits.extend(next(chain))
        near = after(near, *waits) if waits else near
        block = project(plan, side, place, count, own, near, came, legendre, given[k])
        kept.append(block)
        chains.append(line(block, zones, plan))
        next(chains[-1])
    ends = []
    for chain in chains:
        state = None
        for state in chain:
            pass
        ends.append(state)
    for k, end in enumerate(ends):
        place, count = pieces[k][:2]
        mine = finish(count, place, close(*end, zone, plan, half_degrees, kept[-1]))
        result = lax.dynamic_update_slice(result, mine, (place,) + (0,) * 5)
    return result[None]


def line(block, zones, plan):
    widths, places, _ = plan[:3]
    downs, ups = [block[0]], [block[1]]
    came_down, came_up = [], []
    for k in range(zones - 1):
        came_down.append(hop(downs[k], zones - 1 - k, zones - 2 - k))
        came_up.append(hop(ups[k], k, k + 1))
        yield (downs[k], ups[k])
        if k < zones - 2:
            cut = widths[zones - 2 - k]
            downs.append(downs[k][..., cut:] + came_down[k][..., cut:])
            ups.append(ups[k][..., : places[k + 1]] + came_up[k][..., : places[k + 1]])
    yield downs, ups, came_down, came_up


def close(downs, ups, came_down, came_up, zone, plan, half_degrees, last):
    widths, places, _ = plan[:3]
    zones = len(widths)
    downs, ups, came_down, came_up, _ = lax.optimization_barrier(
        (downs, ups, came_down, came_up, last)
    )
    mine = None
    for z in range(zones):
        width = widths[z]
        if z == zones - 1:
            value = ups[0][..., :width]
        else:
            k = zones - 2 - z
            value = downs[k][..., :width] + came_down[k][..., :width]
        if z > 0:
            value = value + came_up[z - 1][..., places[z] : places[z] + width]
        value = jnp.pad(value, ((0, 0), (0, 0), (0, 0), (0, half_degrees - width)))
        mine = value if mine is None else jnp.where(zone == z, value, mine)
    return mine


def solution(mesh):
    in_specs = (P(None, None, None, "lat", "lon"), P("lon", None, "lat", None, None))
    out_specs = P("lon", "lat", None, None, None, None, None)

    return jax.shard_map(local, mesh=mesh, in_specs=in_specs, out_specs=out_specs, check_vma=False)
```

```python
import math

import jax
import jax.numpy as jnp
import numpy as np
from jax import lax
from jax.experimental import pallas as pl
from jax.experimental.pallas import tpu as pltpu
from jax.sharding import PartitionSpec as P


ADIABATIC = 0.286
LANES = 128
SPLIT = ((1, 1, 2), (2, 1, 1))
ROWS_CONTRACTED = (((1,), (1,)), ((), ()))


def tendency_kernel(grid_ref, high_ref, low_ref, scratch):
    pairs = grid_ref.shape[3]
    pieces = grid_ref.shape[4] // LANES

    def field(n):
        return [grid_ref[n, 0, h].astype(jnp.float32) for h in range(2)]

    u, v, zeta, div, temp, hum, temp_x, temp_y, hum_x, hum_y, press_x, press_y = [
        field(n) for n in range(12)
    ]
    formulas = [
        lambda h: zeta[h] * v[h] - temp[h] * press_x[h],
        lambda h: -zeta[h] * u[h] - temp[h] * press_y[h],
        lambda h: u[h] * v[h],
        lambda h: -(u[h] * temp_x[h] + v[h] * temp_y[h]) + ADIABATIC * temp[h] * div[h],
        lambda h: -(u[h] * hum_x[h] + v[h] * hum_y[h]) - hum[h] * div[h],
        lambda h: u[h] * temp[h],
        lambda h: v[h] * temp[h],
        lambda h: v[h] * hum[h],
    ]
    for t, formula in enumerate(formulas):
        north, south = formula(0), formula(1)
        even, odd = north + south, north - south
        for piece in range(pieces):
            lanes = slice(piece * LANES, (piece + 1) * LANES)
            place = t * pieces + piece
            scratch[place, pl.ds(0, pairs, stride=2), :] = even[:, lanes]
            scratch[place, pl.ds(1, pairs, stride=2), :] = odd[:, lanes]
            whole = scratch[place]
            high = whole.astype(jnp.bfloat16)
            high_ref[t, 0, :, lanes] = high
            low_ref[t, 0, :, lanes] = (whole - high.astype(jnp.float32)).astype(jnp.bfloat16)


def folded_tendencies(grid):
    fields, levels, hemispheres, pairs, longitudes = grid.shape
    width = min(256, longitudes)
    shape = jax.ShapeDtypeStruct((8, levels, 2 * pairs, longitudes), jnp.bfloat16)
    high, low = pl.pallas_call(
        tendency_kernel,
        grid=(levels, longitudes // width),
        in_specs=[
            pl.BlockSpec((fields, 1, hemispheres, pairs, width), lambda l, x: (0, l, 0, 0, x))
        ],
        out_specs=[pl.BlockSpec((8, 1, 2 * pairs, width), lambda l, x: (0, l, 0, x))] * 2,
        out_shape=(shape, shape),
        scratch_shapes=[pltpu.VMEM((8 * width // LANES, 2 * pairs, LANES), jnp.float32)],
        cost_estimate=pl.CostEstimate(
            flops=4 * grid.size, bytes_accessed=5 * grid.size, transcendentals=0
        ),
        name="tendencies",
    )(grid)
    rows = 8 * levels * 2 * pairs
    return high.reshape(rows, longitudes), low.reshape(rows, longitudes)


def product3(phase_high, phase_low, high, low):
    def one(a, b):
        return lax.dot_general(a, b, ROWS_CONTRACTED, preferred_element_type=jnp.float32)

    return one(phase_high, high) + (one(phase_high, low) + one(phase_low, high))


def first_fourier_kernel(ph_ref, pl_ref, high_ref, low_ref, out_ref):
    out_ref[...] = product3(ph_ref[...], pl_ref[...], high_ref[...], low_ref[...])


def second_fourier_kernel(ph_ref, pl_ref, high_ref, low_ref, came_ref, *out_refs):
    total = product3(ph_ref[...], pl_ref[...], high_ref[...], low_ref[...]) + came_ref[...]
    start = 0
    for out_ref in out_refs:
        rows = out_ref.shape[0]
        out_ref[...] = total[start : start + rows]
        start += rows


def fourier(phases, tendencies, came=None, parts=()):
    high, low = tendencies
    orders, longitudes = phases[0].shape
    rows = high.shape[0]
    block = min(512, rows)
    whole = pl.BlockSpec((orders, longitudes), lambda r: (0, 0))
    part = pl.BlockSpec((block, longitudes), lambda r: (r, 0))

    def columns(count):
        return pl.BlockSpec((count, block), lambda r: (0, r))

    cost = pl.CostEstimate(
        flops=6 * orders * longitudes * rows,
        bytes_accessed=4 * rows * (longitudes + orders),
        transcendentals=0,
    )
    if came is None:
        return pl.pallas_call(
            first_fourier_kernel,
            grid=(rows // block,),
            in_specs=[whole, whole, part, part],
            out_specs=columns(orders),
            out_shape=jax.ShapeDtypeStruct((orders, rows), jnp.float32),
            cost_estimate=cost,
            name="fourier_first",
        )(*phases, high, low)
    return pl.pallas_call(
        second_fourier_kernel,
        grid=(rows // block,),
        in_specs=[whole, whole, part, part, columns(orders)],
        out_specs=[columns(count) for count in parts],
        out_shape=[jax.ShapeDtypeStruct((count, rows), jnp.float32) for count in parts],
        cost_estimate=cost,
        name="fourier_second",
    )(*phases, high, low, came)


def legendre_kernel(
    sent, depth, last, parity_ref, zone_ref, tile_ref, place_ref, near_ref, came_ref, weights_ref, *rest
):
    folded = rest[-1]
    step = pl.program_id(0)
    count = near_ref.shape[0] // 2
    span = 2 * depth
    batch = near_ref.shape[1] // span
    width = weights_ref.shape[4]

    @pl.when(tile_ref[step] == 0)
    def _():
        total = near_ref[...] + came_ref[...]
        rows = total.reshape(2 * count, batch, span).astype(jnp.bfloat16)
        parity = lax.broadcasted_iota(jnp.int32, (2 * batch, span), 1) % 2
        for r in range(count):
            both = jnp.concatenate([rows[r], rows[count + r]], 0)
            zero = jnp.zeros_like(both)
            folded[r, : 2 * batch] = jnp.where(parity == 0, both, zero)
            folded[r, 2 * batch :] = jnp.where(parity == 1, both, zero)

    start = pl.multiple_of(place_ref[step], LANES)
    values = []
    for r in range(count):
        weights = weights_ref[0, r].reshape(span, width)
        value = jnp.dot(folded[r], weights, preferred_element_type=jnp.float32)
        values += [(r, e, value[e * 2 * batch : (e + 1) * 2 * batch]) for e in range(2)]
    if sent:
        for r, e, value in values:
            rest[0][r, e, :, pl.ds(start, width)] = value
        return
    add_ref, down_ref, up_ref = rest[:3]
    skip = add_ref.shape[3] - down_ref.shape[3]
    sums = [(r, e, value + add_ref[r, e, :, pl.ds(start, width)]) for r, e, value in values]

    @pl.when(zone_ref[step] < last)
    def _():
        for r, e, value in sums:
            down_ref[r, e, :, pl.ds(pl.multiple_of(start - skip, LANES), width)] = value

    @pl.when(zone_ref[step] > 0)
    def _():
        for r, e, value in sums:
            up_ref[r, e, :, pl.ds(start, width)] = value


def degree_plan(zones, half_degrees):
    widths = [-(-(half_degrees - half_degrees * z // zones) // LANES) * LANES for z in range(zones)]
    tile = min(2 * LANES, half_degrees)
    order = list(range(zones))[::-1]
    places, start = [0] * zones, 0
    for z in order:
        places[z] = start
        start += widths[z]
    steps = [(z, k, places[z] + k * tile) for z in order for k in range(-(-widths[z] // tile))]
    return widths, places, start, tile, np.array(steps, np.int32)


def project(plan, parity, place, count, own, near, came, weights, add=None):
    widths, places, total, tile, steps = plan
    zones = len(widths)
    depth = weights.shape[2]
    rows = near.shape[1]
    batch = rows // (2 * depth)
    first = 0 if add is not None else 1

    def rows_of(step, parity, zone, tile_, place_):
        return (first * zones + zone[step], 0)

    def weights_of(step, parity, zone, tile_, place_):
        return (0, (2 * zone[step] + parity[0]) * (own // count) + place // count, 0, 0, tile_[step])

    def lanes(width):
        return pl.BlockSpec((count, 2, 2 * batch, width), lambda step, *_: (0, 0, 0, 0))

    kept = [total - widths[-1], places[0] + tile - LANES]
    outs = [total] if add is None else kept
    in_specs = [
        pl.BlockSpec((2 * count, rows), rows_of),
        pl.BlockSpec((2 * count, rows), rows_of),
        pl.BlockSpec((1, count, depth, 2, tile), weights_of),
    ]
    operands = [near, came, weights]
    if add is not None:
        in_specs.append(lanes(total))
        operands.append(add)

    def kernel(*refs):
        legendre_kernel(add is None, depth, zones - 1, *refs)

    cells = len(steps) * count * tile
    return pl.pallas_call(
        kernel,
        grid_spec=pltpu.PrefetchScalarGridSpec(
            num_scalar_prefetch=4,
            grid=(len(steps),),
            in_specs=in_specs,
            out_specs=[lanes(width) for width in outs],
            scratch_shapes=[pltpu.VMEM((count, 4 * batch, 2 * depth), jnp.bfloat16)],
        ),
        out_shape=[
            jax.ShapeDtypeStruct((count, 2, 2 * batch, width), jnp.float32) for width in outs
        ],
        cost_estimate=pl.CostEstimate(
            flops=4 * cells * 4 * batch * depth,
            bytes_accessed=4 * cells * depth + 8 * count * batch * total,
            transcendentals=0,
        ),
        name="legendre_kept" if add is not None else "legendre_sent",
    )(parity.astype(jnp.int32).reshape(1), *[jnp.asarray(steps[:, k]) for k in range(3)], *operands)


def hop(value, source, target):
    pairs = [(2 * source + x, 2 * target + x) for x in range(2)]
    return lax.ppermute(value, "lat", pairs)


def after(value, *earlier):
    return lax.optimization_barrier((value, *earlier))[0]


def sizes(own):
    unit = own // 8
    if unit % 4:
        return [[own]]
    return [[unit * k for k in group] for group in SPLIT]


def local(grid, legendre):
    lon_count, lat_count = lax.axis_size("lon"), lax.axis_size("lat")
    lon, lat = lax.axis_index("lon"), lax.axis_index("lat")
    levels, longitudes = grid.shape[1], grid.shape[4]
    nlon = longitudes * lon_count
    per, half_degrees = legendre.shape[1], legendre.shape[4]
    own, zones = per // lat_count, lat_count // 2
    waves = per * lon_count
    side, zone = lat % 2, lat // 2
    plan = degree_plan(zones, half_degrees)
    widths, places, total = plan[:3]

    tendencies = folded_tendencies(grid)

    longitude = lon * longitudes + lax.iota(jnp.int32, longitudes)

    def table(wavenumbers, scale):
        product = wavenumbers[..., None] * longitude % nlon
        angles = product.astype(jnp.float32) * (2.0 * math.pi / nlon)
        return jnp.cos(angles) * scale, jnp.sin(angles) * scale

    bands = jnp.stack([2 * lax.iota(jnp.int32, zones) + (side ^ k) for k in range(2)], 0)
    coarse = table(lon_count * own * bands.reshape(-1), 1.0)
    keep = list(range(lon_count - 2, -1, -2))
    halves = [keep[: len(keep) // 2], keep[len(keep) // 2 :]]

    steps = lon_count * lax.iota(jnp.int32, own)
    rels = jnp.stack([lon ^ rel for rel in range(lon_count)])
    cos, sin = table(rels[:, None] + steps, 1.0 / math.sqrt(nlon))

    def phases(bit, chunks):
        blocks = []
        for some in halves:
            for place, count in chunks:
                def fine(values):
                    return jnp.stack([values[rel | bit, place : place + count] for rel in some])

                first = jnp.concatenate([fine(cos), -fine(sin)], 1)[:, None]
                second = jnp.concatenate([fine(sin), fine(cos)], 1)[:, None]
                both = coarse[0][:, None] * first - coarse[1][:, None] * second
                blocks.append(both.reshape(-1, longitudes))
        both = jnp.concatenate(blocks, 0)
        top = lax.reduce_precision(both, 8, 7)
        return top.astype(jnp.bfloat16), (both - top).astype(jnp.bfloat16)

    def lon_swap(value, bit):
        return lax.ppermute(value, "lon", [(i, i ^ bit) for i in range(lon_count)])

    groups, place = [], 0
    for group in sizes(own):
        chunks = []
        for count in group:
            chunks.append((place, count))
            place += count
        groups.append(chunks)

    swapped, before = [], None
    for chunks in groups:
        here = tendencies if before is None else (after(tendencies[0], before), tendencies[1])
        ready = phases(1, chunks)
        before = fourier(ready, here)
        swapped.append(lon_swap(before, 1))
    pieces = []
    for chunks, came in zip(groups, swapped):
        parts = [len(keep) // 2 * 4 * zones * count for _, count in chunks] * 2
        here = (after(tendencies[0], before), tendencies[1])
        ready = phases(0, chunks)
        blocks = fourier(ready, here, came, parts)
        before = blocks[-1]
        for k, (place, count) in enumerate(chunks):
            far, near = blocks[k], blocks[len(chunks) + k]
            bit = lon_count // 2
            while bit > 2:
                near = near + lon_swap(far, bit)
                rows = near.shape[0] // 2
                far, near = near[:rows], near[rows:]
                bit //= 2
            pieces.append((place, count, near, lon_swap(far, bit)))

    result = None
    given, chains, kept = [None] * len(pieces), [], []

    def send(k):
        place, count, near, came = pieces[k]
        if k > 1:
            near = after(near, *kept[k - 2])
        (value,) = project(plan, 1 - side, place, count, own, near, came, legendre)
        given[k] = lax.ppermute(value, "lat", [(i, i ^ 1) for i in range(lat_count)])

    rounds = max(zones - 1, 1)
    for k, (place, count, near, came) in enumerate(pieces):
        if k == 0:
            send(0)
        if k + 1 < len(pieces):
            send(k + 1)
        waits = []
        for number, chain in enumerate(chains):
            if 2 <= k - number <= rounds:
                waits.extend(next(chain))
        near = after(near, *waits) if waits else near
        block = project(plan, side, place, count, own, near, came, legendre, given[k])
        kept.append(block)
        chains.append(line(block, zones, plan))
        next(chains[-1])
    ends = []
    for chain in chains:
        state = None
        for state in chain:
            pass
        ends.append(state)
    for k, end in enumerate(ends):
        place, count = pieces[k][:2]
        base = lon + lon_count * (lat * own + place)
        shape = (own, 8, levels, 2, 2, half_degrees)
        result = close(end, kept[-1], zone, base, lon_count, waves, plan, place, shape, result)
    return result[None]


def line(block, zones, plan):
    widths, places, _ = plan[:3]
    downs, ups = [block[0]], [block[1]]
    came_down, came_up = [], []
    for k in range(zones - 1):
        came_down.append(hop(downs[k], zones - 1 - k, zones - 2 - k))
        came_up.append(hop(ups[k], k, k + 1))
        yield (downs[k], ups[k])
        if k < zones - 2:
            cut = widths[zones - 2 - k]
            downs.append(downs[k][..., cut:] + came_down[k][..., cut:])
            ups.append(ups[k][..., : places[k + 1]] + came_up[k][..., : places[k + 1]])
    yield downs, ups, came_down, came_up


def close_kernel(zones, tiles, stride, waves, fresh, zone_ref, base_ref, *refs):
    refs = refs if fresh else refs[1:]
    hops = zones - 1
    downs, came_down = refs[:hops], refs[hops : 2 * hops]
    up, came_up = refs[2 * hops], refs[2 * hops + 1 : 3 * hops + 1]
    out_ref, total = refs[-2:]
    tile = pl.program_id(0)
    for z in range(zones):
        @pl.when((zone_ref[0] == z) & (tile < tiles[z]))
        def _():
            if z == hops:
                value = up[...]
            else:
                value = downs[hops - 1 - z][...] + came_down[hops - 1 - z][...]
            if z > 0:
                value = value + came_up[z - 1][...]
            total[...] = value

        @pl.when((zone_ref[0] == z) & (tile >= tiles[z]))
        def _():
            total[...] = jnp.zeros_like(total)

    count, _, rows, width = total.shape
    batch = rows // 2
    fields, levels = out_ref.shape[1:3]
    lane = tile * width + lax.broadcasted_iota(jnp.int32, (batch, width), 1)
    for r in range(count):
        for e in range(2):
            inside = 2 * lane + (base_ref[0] + stride * r + e) < waves
            for c in range(2):
                value = total[r, e, c * batch : (c + 1) * batch]
                value = jnp.where(inside, value, jnp.zeros_like(value))
                out_ref[r, :, :, c, e, :] = value.reshape(fields, levels, width)


def close(end, last, zone, base, stride, waves, plan, place, shape, result):
    widths, places, _ = plan[:3]
    zones = len(widths)
    hops = zones - 1
    downs, ups, came_down, came_up, _ = lax.optimization_barrier((*end, last))
    arrays = [*downs, *came_down, ups[0], *came_up]
    users = [hops - 1 - k for k in range(hops)] * 2 + [hops] + [k + 1 for k in range(hops)]
    starts = [0] * (2 * hops + 1) + [places[k + 1] // LANES for k in range(hops)]
    count, _, rows, _ = arrays[0].shape

    def spec(user, start):
        most = start + widths[user] // LANES - 1

        def index(tile, zone_ref, base_ref):
            return (0, 0, 0, jnp.where(zone_ref[0] == user, jnp.minimum(start + tile, most), 0))

        return pl.BlockSpec((count, 2, rows, LANES), index)

    in_specs = [spec(user, start) for user, start in zip(users, starts)]
    scalars = [zone.astype(jnp.int32).reshape(1), base.astype(jnp.int32).reshape(1)]
    aliases = {}
    if result is not None:
        in_specs = [pl.BlockSpec(memory_space=pl.ANY)] + in_specs
        arrays = [result] + arrays
        aliases = {2: 0}
    fresh = result is None
    tiles = [width // LANES for width in widths]

    def kernel(*refs):
        close_kernel(zones, tiles, stride, waves, fresh, *refs)

    block = (count,) + shape[1:-1] + (LANES,)
    return pl.pallas_call(
        kernel,
        grid_spec=pltpu.PrefetchScalarGridSpec(
            num_scalar_prefetch=2,
            grid=(shape[-1] // LANES,),
            in_specs=in_specs,
            out_specs=pl.BlockSpec(block, lambda tile, *_: (place // count, 0, 0, 0, 0, tile)),
            scratch_shapes=[pltpu.VMEM((count, 2, rows, LANES), jnp.float32)],
        ),
        out_shape=jax.ShapeDtypeStruct(shape, jnp.float32),
        input_output_aliases=aliases,
        cost_estimate=pl.CostEstimate(
            flops=count * 2 * rows * shape[-1],
            bytes_accessed=16 * count * 2 * rows * shape[-1],
            transcendentals=0,
        ),
        name="close",
    )(*scalars, *arrays)


def solution(mesh):
    in_specs = (P(None, None, None, "lat", "lon"), P("lon", None, "lat", None, None))
    out_specs = P("lon", "lat", None, None, None, None, None)

    return jax.shard_map(local, mesh=mesh, in_specs=in_specs, out_specs=out_specs, check_vma=False)
```

```python
import math

import jax
import jax.numpy as jnp
import numpy as np
from jax import lax
from jax.experimental import pallas as pl
from jax.experimental.pallas import tpu as pltpu
from jax.sharding import PartitionSpec as P


ADIABATIC = 0.286
LANES = 128
SPLIT = ((1, 1), (2,), (2, 1, 1))
ROWS_CONTRACTED = (((1,), (1,)), ((), ()))


def tendency_kernel(grid_ref, high_ref, low_ref, scratch):
    pairs = grid_ref.shape[3]
    pieces = grid_ref.shape[4] // LANES

    def field(n):
        return [grid_ref[n, 0, h].astype(jnp.float32) for h in range(2)]

    u, v, zeta, div, temp, hum, temp_x, temp_y, hum_x, hum_y, press_x, press_y = [
        field(n) for n in range(12)
    ]
    formulas = [
        lambda h: zeta[h] * v[h] - temp[h] * press_x[h],
        lambda h: -zeta[h] * u[h] - temp[h] * press_y[h],
        lambda h: u[h] * v[h],
        lambda h: -(u[h] * temp_x[h] + v[h] * temp_y[h]) + ADIABATIC * temp[h] * div[h],
        lambda h: -(u[h] * hum_x[h] + v[h] * hum_y[h]) - hum[h] * div[h],
        lambda h: u[h] * temp[h],
        lambda h: v[h] * temp[h],
        lambda h: v[h] * hum[h],
    ]
    for t, formula in enumerate(formulas):
        north, south = formula(0), formula(1)
        even, odd = north + south, north - south
        for piece in range(pieces):
            lanes = slice(piece * LANES, (piece + 1) * LANES)
            place = t * pieces + piece
            scratch[place, pl.ds(0, pairs, stride=2), :] = even[:, lanes]
            scratch[place, pl.ds(1, pairs, stride=2), :] = odd[:, lanes]
            whole = scratch[place]
            high = whole.astype(jnp.bfloat16)
            high_ref[t, 0, :, lanes] = high
            low_ref[t, 0, :, lanes] = (whole - high.astype(jnp.float32)).astype(jnp.bfloat16)


def folded_tendencies(grid):
    fields, levels, hemispheres, pairs, longitudes = grid.shape
    width = min(256, longitudes)
    shape = jax.ShapeDtypeStruct((8, levels, 2 * pairs, longitudes), jnp.bfloat16)
    high, low = pl.pallas_call(
        tendency_kernel,
        grid=(levels, longitudes // width),
        in_specs=[
            pl.BlockSpec((fields, 1, hemispheres, pairs, width), lambda l, x: (0, l, 0, 0, x))
        ],
        out_specs=[pl.BlockSpec((8, 1, 2 * pairs, width), lambda l, x: (0, l, 0, x))] * 2,
        out_shape=(shape, shape),
        scratch_shapes=[pltpu.VMEM((8 * width // LANES, 2 * pairs, LANES), jnp.float32)],
        cost_estimate=pl.CostEstimate(
            flops=4 * grid.size, bytes_accessed=5 * grid.size, transcendentals=0
        ),
        name="tendencies",
    )(grid)
    rows = 8 * levels * 2 * pairs
    return high.reshape(rows, longitudes), low.reshape(rows, longitudes)


def product3(phase_high, phase_low, high, low):
    def one(a, b):
        return lax.dot_general(a, b, ROWS_CONTRACTED, preferred_element_type=jnp.float32)

    return one(phase_high, high) + (one(phase_high, low) + one(phase_low, high))


def first_fourier_kernel(ph_ref, pl_ref, high_ref, low_ref, out_ref):
    out_ref[...] = product3(ph_ref[...], pl_ref[...], high_ref[...], low_ref[...])


def second_fourier_kernel(ph_ref, pl_ref, high_ref, low_ref, came_ref, *out_refs):
    total = product3(ph_ref[...], pl_ref[...], high_ref[...], low_ref[...]) + came_ref[...]
    start = 0
    for out_ref in out_refs:
        rows = out_ref.shape[0]
        out_ref[...] = total[start : start + rows]
        start += rows


def fourier(phases, tendencies, came=None, parts=()):
    high, low = tendencies
    orders, longitudes = phases[0].shape
    rows = high.shape[0]
    block = min(512, rows)
    whole = pl.BlockSpec((orders, longitudes), lambda r: (0, 0))
    part = pl.BlockSpec((block, longitudes), lambda r: (r, 0))

    def columns(count):
        return pl.BlockSpec((count, block), lambda r: (0, r))

    cost = pl.CostEstimate(
        flops=6 * orders * longitudes * rows,
        bytes_accessed=4 * rows * (longitudes + orders),
        transcendentals=0,
    )
    if came is None:
        return pl.pallas_call(
            first_fourier_kernel,
            grid=(rows // block,),
            in_specs=[whole, whole, part, part],
            out_specs=columns(orders),
            out_shape=jax.ShapeDtypeStruct((orders, rows), jnp.float32),
            cost_estimate=cost,
            name="fourier_first",
        )(*phases, high, low)
    return pl.pallas_call(
        second_fourier_kernel,
        grid=(rows // block,),
        in_specs=[whole, whole, part, part, columns(orders)],
        out_specs=[columns(count) for count in parts],
        out_shape=[jax.ShapeDtypeStruct((count, rows), jnp.float32) for count in parts],
        cost_estimate=cost,
        name="fourier_second",
    )(*phases, high, low, came)


def legendre_kernel(
    sent, depth, last, parity_ref, zone_ref, tile_ref, place_ref, near_ref, came_ref, weights_ref, *rest
):
    folded = rest[-1]
    step = pl.program_id(0)
    count = near_ref.shape[0] // 2
    span = 2 * depth
    batch = near_ref.shape[1] // span
    width = weights_ref.shape[4]

    @pl.when(tile_ref[step] == 0)
    def _():
        total = near_ref[...] + came_ref[...]
        rows = total.reshape(2 * count, batch, span).astype(jnp.bfloat16)
        parity = lax.broadcasted_iota(jnp.int32, (2 * batch, span), 1) % 2
        for r in range(count):
            both = jnp.concatenate([rows[r], rows[count + r]], 0)
            zero = jnp.zeros_like(both)
            folded[r, : 2 * batch] = jnp.where(parity == 0, both, zero)
            folded[r, 2 * batch :] = jnp.where(parity == 1, both, zero)

    start = pl.multiple_of(place_ref[step], LANES)
    values = []
    for r in range(count):
        weights = weights_ref[0, r].reshape(span, width)
        value = jnp.dot(folded[r], weights, preferred_element_type=jnp.float32)
        values += [(r, e, value[e * 2 * batch : (e + 1) * 2 * batch]) for e in range(2)]
    if sent:
        for r, e, value in values:
            rest[0][r, e, :, pl.ds(start, width)] = value
        return
    add_ref, down_ref, up_ref = rest[:3]
    skip = add_ref.shape[3] - down_ref.shape[3]
    sums = [(r, e, value + add_ref[r, e, :, pl.ds(start, width)]) for r, e, value in values]

    @pl.when(zone_ref[step] < last)
    def _():
        for r, e, value in sums:
            down_ref[r, e, :, pl.ds(pl.multiple_of(start - skip, LANES), width)] = value

    @pl.when(zone_ref[step] > 0)
    def _():
        for r, e, value in sums:
            up_ref[r, e, :, pl.ds(start, width)] = value


def degree_plan(zones, half_degrees):
    widths = [-(-(half_degrees - half_degrees * z // zones) // LANES) * LANES for z in range(zones)]
    tile = min(2 * LANES, half_degrees)
    order = list(range(zones))[::-1]
    places, start = [0] * zones, 0
    for z in order:
        places[z] = start
        start += widths[z]
    steps = [(z, k, places[z] + k * tile) for z in order for k in range(-(-widths[z] // tile))]
    return widths, places, start, tile, np.array(steps, np.int32)


def project(plan, parity, place, count, own, near, came, weights, add=None):
    widths, places, total, tile, steps = plan
    zones = len(widths)
    depth = weights.shape[2]
    rows = near.shape[1]
    batch = rows // (2 * depth)
    first = 0 if add is not None else 1

    def rows_of(step, parity, zone, tile_, place_):
        return (first * zones + zone[step], 0)

    def weights_of(step, parity, zone, tile_, place_):
        return (0, (2 * zone[step] + parity[0]) * (own // count) + place // count, 0, 0, tile_[step])

    def lanes(width):
        return pl.BlockSpec((count, 2, 2 * batch, width), lambda step, *_: (0, 0, 0, 0))

    kept = [total - widths[-1], places[0] + tile - LANES]
    outs = [total] if add is None else kept
    in_specs = [
        pl.BlockSpec((2 * count, rows), rows_of),
        pl.BlockSpec((2 * count, rows), rows_of),
        pl.BlockSpec((1, count, depth, 2, tile), weights_of),
    ]
    operands = [near, came, weights]
    if add is not None:
        in_specs.append(lanes(total))
        operands.append(add)

    def kernel(*refs):
        legendre_kernel(add is None, depth, zones - 1, *refs)

    cells = len(steps) * count * tile
    return pl.pallas_call(
        kernel,
        grid_spec=pltpu.PrefetchScalarGridSpec(
            num_scalar_prefetch=4,
            grid=(len(steps),),
            in_specs=in_specs,
            out_specs=[lanes(width) for width in outs],
            scratch_shapes=[pltpu.VMEM((count, 4 * batch, 2 * depth), jnp.bfloat16)],
        ),
        out_shape=[
            jax.ShapeDtypeStruct((count, 2, 2 * batch, width), jnp.float32) for width in outs
        ],
        cost_estimate=pl.CostEstimate(
            flops=4 * cells * 4 * batch * depth,
            bytes_accessed=4 * cells * depth + 8 * count * batch * total,
            transcendentals=0,
        ),
        name="legendre_kept" if add is not None else "legendre_sent",
    )(parity.astype(jnp.int32).reshape(1), *[jnp.asarray(steps[:, k]) for k in range(3)], *operands)


def hop(value, source, target):
    pairs = [(2 * source + x, 2 * target + x) for x in range(2)]
    return lax.ppermute(value, "lat", pairs)


def after(value, *earlier):
    return lax.optimization_barrier((value, *earlier))[0]


def sizes(own):
    unit = own // 8
    if unit % 4:
        return [[own]]
    return [[unit * k for k in group] for group in SPLIT]


def local(grid, legendre):
    lon_count, lat_count = lax.axis_size("lon"), lax.axis_size("lat")
    lon, lat = lax.axis_index("lon"), lax.axis_index("lat")
    levels, longitudes = grid.shape[1], grid.shape[4]
    nlon = longitudes * lon_count
    per, half_degrees = legendre.shape[1], legendre.shape[4]
    own, zones = per // lat_count, lat_count // 2
    waves = per * lon_count
    side, zone = lat % 2, lat // 2
    plan = degree_plan(zones, half_degrees)
    widths, places, total = plan[:3]

    tendencies = folded_tendencies(grid)

    longitude = lon * longitudes + lax.iota(jnp.int32, longitudes)

    def table(wavenumbers, scale, turn=0):
        product = (wavenumbers[..., None] * longitude + jnp.asarray(turn)[..., None]) % nlon
        angles = product.astype(jnp.float32) * (2.0 * math.pi / nlon)
        return jnp.cos(angles) * scale, jnp.sin(angles) * scale

    bands = jnp.stack([2 * lax.iota(jnp.int32, zones) + (side ^ k) for k in range(2)], 0)
    coarse = table(lon_count * own * bands.reshape(-1), 1.0)
    keep = list(range(lon_count - 2, -1, -2))
    halves = [keep[: len(keep) // 2], keep[len(keep) // 2 :]]

    groups, place = [], 0
    for group in sizes(own):
        chunks = []
        for count in group:
            chunks.append((place, count))
            place += count
        groups.append(chunks)

    spots = [
        (start + r, part)
        for chunks in groups
        for start, count in chunks
        for part in range(2)
        for r in range(count)
    ]
    steps = jnp.asarray(np.array([lon_count * r for r, _ in spots], np.int32))
    quarters = jnp.asarray(np.array([part * (nlon // 4) for _, part in spots], np.int32))
    rels = jnp.stack([lon ^ rel for rel in range(lon_count)])
    cos, sin = table(rels[:, None] + steps, 1.0 / math.sqrt(nlon), quarters)

    def phases(bit, chunks):
        blocks = []
        for some in halves:
            for place, count in chunks:
                rows = slice(2 * place, 2 * (place + count))
                for rel in some:
                    first, second = cos[rel | bit, rows], sin[rel | bit, rows]
                    both = coarse[0][:, None] * first - coarse[1][:, None] * second
                    blocks.append(both.reshape(-1, longitudes))
        both = jnp.concatenate(blocks, 0)
        top = lax.reduce_precision(both, 8, 7)
        return top.astype(jnp.bfloat16), (both - top).astype(jnp.bfloat16)

    def lon_swap(value, bit):
        return lax.ppermute(value, "lon", [(i, i ^ bit) for i in range(lon_count)])

    given, chains, kept, pieces, swapped = [], [], [], [], []
    before = []

    def held():
        if not before:
            return tendencies
        return after(tendencies[0], before[-1]), tendencies[1]

    def first(number):
        ready = phases(1, groups[number])
        before.append(fourier(ready, held()))
        swapped.append(lon_swap(before[-1], 1))

    def second(number):
        chunks = groups[number]
        parts = [len(keep) // 2 * 4 * zones * count for _, count in chunks] * 2
        ready = phases(0, chunks)
        blocks = fourier(ready, held(), swapped[number], parts)
        before.append(blocks[-1])
        for k, (place, count) in enumerate(chunks):
            far, near = blocks[k], blocks[len(chunks) + k]
            bit = lon_count // 2
            while bit > 2:
                near = near + lon_swap(far, bit)
                rows = near.shape[0] // 2
                far, near = near[:rows], near[rows:]
                bit //= 2
            pieces.append((place, count, near, lon_swap(far, bit)))

    def send(k):
        place, count, near, came = pieces[k]
        if k > 1 and len(kept) > k - 2:
            near = after(near, *kept[k - 2])
        else:
            near = after(near, before[-1])
        (value,) = project(plan, 1 - side, place, count, own, near, came, legendre)
        before.append(value)
        given.append(lax.ppermute(value, "lat", [(i, i ^ 1) for i in range(lat_count)]))

    first(0)
    second(0)
    for number in range(1, len(groups)):
        first(number)
    send(0)
    for number in range(1, len(groups)):
        second(number)
        if number == 1 and len(pieces) > 1:
            send(1)
    result = None
    rounds = max(zones - 1, 1)
    for k, (place, count, near, came) in enumerate(pieces):
        if k == 0:
            near = after(near, before[-1])
        if len(given) == k + 1 and k + 1 < len(pieces):
            send(k + 1)
        waits = []
        for number, chain in enumerate(chains):
            if 2 <= k - number <= rounds:
                waits.extend(next(chain))
        near = after(near, *waits) if waits else near
        block = project(plan, side, place, count, own, near, came, legendre, given[k])
        kept.append(block)
        chains.append(line(block, zones, plan))
        next(chains[-1])
    ends = []
    for chain in chains:
        state = None
        for state in chain:
            pass
        ends.append(state)
    for k, end in enumerate(ends):
        place, count = pieces[k][:2]
        base = lon + lon_count * (lat * own + place)
        shape = (own, 8, levels, 2, 2, half_degrees)
        result = close(end, kept[-1], zone, base, lon_count, waves, plan, place, shape, result)
    return result[None]


def line(block, zones, plan):
    widths, places, _ = plan[:3]
    downs, ups = [block[0]], [block[1]]
    came_down, came_up = [], []
    for k in range(zones - 1):
        came_down.append(hop(downs[k], zones - 1 - k, zones - 2 - k))
        came_up.append(hop(ups[k], k, k + 1))
        yield (downs[k], ups[k])
        if k < zones - 2:
            cut = widths[zones - 2 - k]
            downs.append(downs[k][..., cut:] + came_down[k][..., cut:])
            ups.append(ups[k][..., : places[k + 1]] + came_up[k][..., : places[k + 1]])
    yield downs, ups, came_down, came_up


def close_kernel(zones, tiles, stride, waves, fresh, zone_ref, base_ref, *refs):
    refs = refs if fresh else refs[1:]
    hops = zones - 1
    downs, came_down = refs[:hops], refs[hops : 2 * hops]
    up, came_up = refs[2 * hops], refs[2 * hops + 1 : 3 * hops + 1]
    out_ref, total = refs[-2:]
    tile = pl.program_id(0)
    for z in range(zones):
        @pl.when((zone_ref[0] == z) & (tile < tiles[z]))
        def _():
            if z == hops:
                value = up[...]
            else:
                value = downs[hops - 1 - z][...] + came_down[hops - 1 - z][...]
            if z > 0:
                value = value + came_up[z - 1][...]
            total[...] = value

        @pl.when((zone_ref[0] == z) & (tile >= tiles[z]))
        def _():
            total[...] = jnp.zeros_like(total)

    count, _, rows, width = total.shape
    batch = rows // 2
    fields, levels = out_ref.shape[1:3]
    lane = tile * width + lax.broadcasted_iota(jnp.int32, (batch, width), 1)
    for r in range(count):
        for e in range(2):
            inside = 2 * lane + (base_ref[0] + stride * r + e) < waves
            for c in range(2):
                value = total[r, e, c * batch : (c + 1) * batch]
                value = jnp.where(inside, value, jnp.zeros_like(value))
                out_ref[r, :, :, c, e, :] = value.reshape(fields, levels, width)


def close(end, last, zone, base, stride, waves, plan, place, shape, result):
    widths, places, _ = plan[:3]
    zones = len(widths)
    hops = zones - 1
    downs, ups, came_down, came_up, _ = lax.optimization_barrier((*end, last))
    arrays = [*downs, *came_down, ups[0], *came_up]
    users = [hops - 1 - k for k in range(hops)] * 2 + [hops] + [k + 1 for k in range(hops)]
    starts = [0] * (2 * hops + 1) + [places[k + 1] // LANES for k in range(hops)]
    count, _, rows, _ = arrays[0].shape

    def spec(user, start):
        most = start + widths[user] // LANES - 1

        def index(tile, zone_ref, base_ref):
            return (0, 0, 0, jnp.where(zone_ref[0] == user, jnp.minimum(start + tile, most), 0))

        return pl.BlockSpec((count, 2, rows, LANES), index)

    in_specs = [spec(user, start) for user, start in zip(users, starts)]
    scalars = [zone.astype(jnp.int32).reshape(1), base.astype(jnp.int32).reshape(1)]
    aliases = {}
    if result is not None:
        in_specs = [pl.BlockSpec(memory_space=pl.ANY)] + in_specs
        arrays = [result] + arrays
        aliases = {2: 0}
    fresh = result is None
    tiles = [width // LANES for width in widths]

    def kernel(*refs):
        close_kernel(zones, tiles, stride, waves, fresh, *refs)

    block = (count,) + shape[1:-1] + (LANES,)
    return pl.pallas_call(
        kernel,
        grid_spec=pltpu.PrefetchScalarGridSpec(
            num_scalar_prefetch=2,
            grid=(shape[-1] // LANES,),
            in_specs=in_specs,
            out_specs=pl.BlockSpec(block, lambda tile, *_: (place // count, 0, 0, 0, 0, tile)),
            scratch_shapes=[pltpu.VMEM((count, 2, rows, LANES), jnp.float32)],
        ),
        out_shape=jax.ShapeDtypeStruct(shape, jnp.float32),
        input_output_aliases=aliases,
        cost_estimate=pl.CostEstimate(
            flops=count * 2 * rows * shape[-1],
            bytes_accessed=16 * count * 2 * rows * shape[-1],
            transcendentals=0,
        ),
        name="close",
    )(*scalars, *arrays)


def solution(mesh):
    in_specs = (P(None, None, None, "lat", "lon"), P("lon", None, "lat", None, None))
    out_specs = P("lon", "lat", None, None, None, None, None)

    return jax.shard_map(local, mesh=mesh, in_specs=in_specs, out_specs=out_specs, check_vma=False)
```
